32 devices in a mesh: refl: 4 (over y, x), grid: 8 (over z, core).
Axes of the slice: x: 2, y: 2, z: 4, core: 2. Of those that a mesh axis runs over, the one named last changes fastest.
Arguments:
- density: bfloat16 [2, 256, 256, 256], P(None, 'grid'), may hold values from -6 to 6
- displacement: bfloat16 [3, 256, 256, 256], P(None, 'grid'), may hold values from -0.8984375 to 0.8984375
- support: int32 [256, 256, 256], P('grid'), may hold values 0 or 1
- millers: int32 [4, 3], replicated, may hold values from -3 to 3
- amplitude: float32 [4, 256, 256, 256], P('refl', None, 'grid'), may hold values from 0.1 to 3
Outputs:
- grad_density: float32 [2, 256, 256, 256], P(None, 'grid', 'refl')
- grad_displacement: float32 [3, 256, 256, 256], P(None, 'grid', 'refl')
The draws below stay inside these ranges and needn't reach their ends.
All inputs are finite; a program needn't handle non-finite values. No bound on the sum of `support` on one device may be relied on, other than what follows from the above.
Results may differ from the reference program's by a relative error of at most 0.00065.
Values sent between devices are 32-bit elements; how exact they have to be, the bound alone decides.
A program may use at most 192 MiB of HBM per device.

```python
import math
import jax
import jax.numpy as jnp
from jax import lax

N = 256
NREF = 4


def set_ends(values, own_key, low, high):
    place = [jax.random.randint(jax.random.fold_in(own_key, axis), (), 0, length) for axis, length in enumerate(values.shape)]
    widest = values.shape.index(max(values.shape))
    next_to = place[:widest] + [(place[widest] + 1) % values.shape[widest]] + place[widest + 1:]
    return values.at[tuple(place)].set(low).at[tuple(next_to)].set(high)


def levels(stream_key, extent, split, smallest, top_value):
    gain, own = 1.0, jax.random.fold_in(stream_key, 6)
    for dim, shards_of in split:
        heights = jnp.exp(jax.random.uniform(jax.random.fold_in(own, dim), (shards_of,), jnp.float32, smallest / len(split), top_value / len(split)))
        gain = gain * jnp.repeat(heights, extent[dim] // shards_of).reshape([-1 if axis == dim else 1 for axis in range(len(extent))])
    return gain


def gaussian(stream_key, shape, width, bound, pieces=(), dtype=jnp.bfloat16):
    gain = levels(stream_key, shape, pieces, -0.22, 0.18) if pieces else 1.0
    values = jax.random.normal(stream_key, shape, jnp.float32) * width * gain
    return jnp.minimum(jnp.maximum(values, -bound), bound).astype(dtype)


def setup_inputs(seed: int = 0) -> dict:
    streams_of = jax.random.split(jax.random.key(seed), 6)
    density = gaussian(streams_of[0], (2, N, N, N), 1.0, 6.0, ((1, 8),))
    displacement = gaussian(streams_of[1], (3, N, N, N), 0.15, 0.8984375, ((1, 8),))
    support = set_ends((jax.random.randint(streams_of[2], (N, N, N), 0, 4) < 3).astype(jnp.int32), jax.random.fold_in(streams_of[2], 1), 0, 1)
    millers = set_ends(jax.random.randint(streams_of[3], (NREF, 3), -3, 4), jax.random.fold_in(streams_of[3], 1), -3, 3).astype(jnp.int32)
    amplitude = jnp.clip(jnp.exp(math.log(3.0) - 3.4011974 * jax.random.uniform(streams_of[4], (NREF, N, N, N), jnp.float32) ** levels(streams_of[4], (NREF, N, N, N), ((0, 4), (2, 8)), -0.2, 0.2)), 0.1, 3.0)
    return {"density": density, "displacement": displacement, "support": support, "millers": millers, "amplitude": amplitude}


def reference(density, displacement, support, millers, amplitude):
    rho_real = density[0].astype(jnp.float32)
    rho_imag = density[1].astype(jnp.float32)
    shift = displacement.astype(jnp.float32)
    mask = support.astype(jnp.float32)
    indices = millers.astype(jnp.float32)
    grad_real = jnp.zeros_like(rho_real)
    grad_imag = jnp.zeros_like(rho_real)
    grad_shift = jnp.zeros_like(shift)
    for refl_index in range(NREF):
        hkl = indices[refl_index]
        phase = (2.0 * math.pi) * (hkl[0] * shift[0] + hkl[1] * shift[1] + hkl[2] * shift[2])
        cosine = jnp.cos(phase)
        sine = jnp.sin(phase)
        obj_real = mask * (rho_real * cosine - rho_imag * sine)
        obj_imag = mask * (rho_real * sine + rho_imag * cosine)
        spectrum = jnp.fft.fftn(lax.complex(obj_real, obj_imag), norm="ortho")
        magnitude = jnp.abs(spectrum)
        resid = spectrum - (amplitude[refl_index] / jnp.maximum(magnitude, 0.5)) * spectrum
        back = jnp.fft.ifftn(resid, norm="ortho")
        back_real = jnp.real(back)
        back_imag = jnp.imag(back)
        grad_real = grad_real + mask * (cosine * back_real + sine * back_imag)
        grad_imag = grad_imag + mask * (cosine * back_imag - sine * back_real)
        twist = obj_real * back_imag - obj_imag * back_real
        grad_shift = grad_shift + hkl[:, None, None, None] * twist[None]
    scale = 1.0 / NREF
    return jnp.stack([grad_real, grad_imag]) * scale, grad_shift * scale
```

```python
import math

import jax
import jax.numpy as jnp
from jax import lax
from jax.sharding import PartitionSpec as P

PREC = lax.Precision.HIGH
FWD = 2
BWD = 4


def dft_tables(length):
    counter = jnp.arange(length, dtype=jnp.int32)
    product = counter[:, None] * counter[None, :] % length
    angles = product.astype(jnp.float32) * (2.0 * math.pi / length)
    factor = 1.0 / math.sqrt(length)
    return (jnp.cos(angles) * factor, jnp.sin(angles) * factor)


def apply(pattern, real, imag, cosine, sine, inverse):
    def dot(a, b):
        return jnp.einsum(pattern, a, b, precision=PREC)

    if inverse:
        return dot(real, cosine) - dot(imag, sine), dot(imag, cosine) + dot(real, sine)
    return dot(real, cosine) + dot(imag, sine), dot(imag, cosine) - dot(real, sine)


def poly(square, coefficients):
    total = jnp.full_like(square, coefficients[-1])
    for value in coefficients[-2::-1]:
        total = total * square + value
    return total


SIN = [(-1) ** k / math.factorial(2 * k + 1) for k in range(7)]
COS = [(-1) ** k / math.factorial(2 * k) for k in range(7)]


def phase(hkl, u0, u1, u2):
    turns = hkl[0] * u0 + hkl[1] * u1 + hkl[2] * u2
    half = (turns - jnp.round(turns)) * math.pi
    square = half * half
    s = half * poly(square, SIN)
    c = poly(square, COS)
    return 1.0 - 2.0 * s * s, 2.0 * s * c


def exchange(block, axis):
    return lax.all_to_all(block, axis, split_axis=0, concat_axis=0, tiled=True)


def partner(me, step, size):
    if size & (size - 1) == 0:
        return me ^ step, me ^ step
    return (me + step) % size, (me + size - step) % size


def scatter(block, axis, size):
    me = lax.axis_index(axis)
    got = []
    for step in range(size):
        piece = lax.dynamic_index_in_dim(block, partner(me, step, size)[0], 0, False)
        if step:
            piece = lax.ppermute(piece, axis, [(i, partner(i, step, size)[0]) for i in range(size)])
        got.append(piece)
    return got


def tie(*values):
    return lax.optimization_barrier(values)


def body(density, displacement, support, millers, amplitude, *, refl, grid):
    total_refl = millers.shape[0]
    nx, ky_own, nz = amplitude.shape[1:]
    x_own, ny, _ = support.shape
    y_own = ny // refl
    indices = millers.astype(jnp.float32)
    me = lax.axis_index("refl")
    cx, sx = dft_tables(nx)
    cy, sy = dft_tables(ny)
    cz, sz = dft_tables(nz)

    hkl = lax.dynamic_index_in_dim(indices, me, 0, False)
    u = displacement.astype(jnp.float32)
    mask = support.astype(jnp.float32)
    c, s = phase(hkl, u[0], u[1], u[2])
    rr, ri = density[0].astype(jnp.float32) * mask, density[1].astype(jnp.float32) * mask
    obj = lax.optimization_barrier((rr * c - ri * s, rr * s + ri * c))
    ar, ai = lax.optimization_barrier(apply("xyz,zk->xyk", *obj, cz, sz, False))

    y_from = me * y_own
    dens = lax.dynamic_slice_in_dim(density, y_from, y_own, 2)
    disp = lax.dynamic_slice_in_dim(displacement, y_from, y_own, 2)
    supp = lax.dynamic_slice_in_dim(support, y_from, y_own, 1)
    senders = [indices[partner(me, step, refl)[1]] for step in range(refl)]

    part = ky_own // FWD
    cyd = cy.reshape(ny, grid, FWD, part)
    syd = sy.reshape(ny, grid, FWD, part)
    arrived, phases = [], None
    for f in range(FWD):
        br, bi = apply("xyk,ydj->dxjk", ar, ai, cyd[:, :, f], syd[:, :, f], False)
        if f == FWD - 1:
            late, _ = tie(disp, arrived[0][0])
            phases = [phase(k, *late.astype(jnp.float32)) for k in senders]
            bi, phases = tie(bi, phases)
        arrived.append([exchange(v, "grid").reshape(nx, part, nz) for v in (br, bi)])
    resid = []
    for f in range(FWD):
        pr, pi = apply("xjk,xm->mjk", *arrived[f], cx, sx, False)
        magnitude = jnp.sqrt(pr * pr + pi * pi)
        amp = amplitude[0, :, f * part : (f + 1) * part]
        keep = 1.0 - amp / jnp.maximum(magnitude, 0.5)
        resid.append(tie(keep * pr, keep * pi))

    sub = x_own // BWD
    cxd = cx.reshape(nx, grid, BWD, sub)
    sxd = sx.reshape(nx, grid, BWD, sub)
    cyr = cy.reshape(ny, refl, y_own)
    syr = sy.reshape(ny, refl, y_own)
    backs, grads, shifts = [], [], []
    for b in range(BWD):
        pieces = [
            apply("mjk,mdx->djxk", *resid[f], cxd[:, :, b], sxd[:, :, b], True) for f in range(FWD)
        ]
        send = jnp.stack([jnp.concatenate([p[i] for p in pieces], axis=1) for i in range(2)], axis=1)
        if b >= 2:
            send, backs[b - 2] = tie(send, backs[b - 2])
        both = exchange(send, "grid")
        er, ei = [both[:, i].reshape(ny, sub, nz) for i in range(2)]
        er, ei = tie(*apply("kxz,kry->rxyz", er, ei, cyr, syr, True))
        backs.append(jnp.stack(apply("rxyk,kz->rxyz", er, ei, cz, sz, True), axis=1))
    for b in range(BWD):
        got = scatter(backs[b], "refl", refl)
        rows = slice(b * sub, (b + 1) * sub)
        scaled = supp[rows].astype(jnp.float32) * (1.0 / total_refl)
        rho_r, rho_i = dens[0, rows].astype(jnp.float32), dens[1, rows].astype(jnp.float32)
        gr = gi = 0.0
        sh = [0.0, 0.0, 0.0]
        for (vr, vi), (c, s), k in zip(got, phases, senders):
            c, s = c[rows], s[rows]
            dr, di = c * vr + s * vi, c * vi - s * vr
            gr, gi = gr + dr, gi + di
            twist = rho_r * di - rho_i * dr
            sh = [sh[i] + k[i] * twist for i in range(3)]
        grads.append(jnp.stack([gr * scaled, gi * scaled]))
        shifts.append(jnp.stack([v * scaled for v in sh]))
    return jnp.concatenate(grads, axis=1), jnp.concatenate(shifts, axis=1)


def solution(mesh):
    refl, grid = mesh.shape["refl"], mesh.shape["grid"]

    def step(*args):
        return body(*args, refl=refl, grid=grid)

    in_specs = (
        P(None, "grid", None, None),
        P(None, "grid", None, None),
        P("grid", None, None),
        P(),
        P("refl", None, "grid", None),
    )
    out_specs = (P(None, "grid", "refl", None), P(None, "grid", "refl", None))
    return jax.shard_map(step, mesh=mesh, in_specs=in_specs, out_specs=out_specs, check_vma=False)
```
